512 devices in a mesh: expert: 32 (over x, y), dp: 16 (over z, core).
Axes of the slice: x: 4, y: 8, z: 8, core: 2. Of those that a mesh axis runs over, the one named last changes fastest.
Arguments:
- frames_in: bfloat16 [32, 2048, 1536], P('expert', 'dp'), may hold values from -6 to 6
- conv_kernel: bfloat16 [31, 1536], replicated, may hold values from -1 to 1
- norm_gain: bfloat16 [1536], replicated, may hold values from 0.099609375 to 1.8984375
- router: bfloat16 [1536, 32], replicated, may hold values from -0.15625 to 0.15625
- w_in: bfloat16 [32, 3072, 1536], P('expert', 'dp'), may hold values from -0.15625 to 0.15625
- w_out: bfloat16 [32, 3072, 1536], P('expert', 'dp'), may hold values from -0.109375 to 0.109375
- routes: int32 [32, 2048, 2], P('expert', 'dp'), may hold values from 0 to 31, all different within a row; in each aligned block of 128 rows (0 to 127, 128 to 255, ..., all dimensions but the last counted through in order) at most 9 rows name the same one
Outputs:
- block_output: bfloat16 [32, 2048, 1536], P('expert', 'dp')
The draws below stay inside these ranges and needn't reach their ends.
Inputs may be any that keep to these rules, and one draw needn't show every extreme that they name: `routes`: each frame names 2 different experts. In each aligned block of 128 frames of an utterance (the frames of one device) no expert is named more than 9 times, a bound that some block reaches.
All inputs are finite; a program needn't handle non-finite values.
Results may differ from the reference program's by a relative error of at most 0.007.
Values may be sent and summed in bfloat16 or wider, within the bound.
No kernel may reach another device: no remote copies, remote signals or barrier semaphores. Data moves between devices by JAX's collectives and lax.ppermute only.
A program may use at most 64 MiB of HBM per device.

```python
import math
import jax
import jax.numpy as jnp
import numpy as np
from jax import lax

D = 1536
FF = 3072
KSIZE = 31
TOP = 2
TOK_DEV = 128
EXPERTS = 32
UTTS = 32
FRAMES = 2048
CAP = 9
N_DP = 16


def steps_of(key, shape, pieces, least, high):
    def one(axis_at, shards_of):
        draws = jax.random.uniform(jax.random.fold_in(jax.random.fold_in(key, 6), axis_at), (shards_of,), jnp.float32, least / len(pieces), high / len(pieces))
        return jnp.repeat(jnp.exp(draws), shape[axis_at] // shards_of).reshape((-1,) + (1,) * (len(shape) - axis_at - 1))

    gain = one(*pieces[0])
    for cut in pieces[1:]:
        gain = gain * one(*cut)
    return gain


def shared_out(own_key, own, number, rows, amount, top, reach, lean):
    sequence = jax.random.permutation(own_key, amount)
    crowded, usual = load_shares(amount, rows * top, reach, lean, True), load_shares(amount, rows * top, reach, lean, False)
    places = jnp.arange(amount)

    def named(lengths, turn):
        used = int((lengths > 0).sum())
        fixed = max(1, used // 4)
        shifted = fixed + (places - fixed + turn * (used - fixed)) % max(1, amount - fixed)
        return jnp.zeros((amount,), jnp.int32).at[sequence[jnp.where(places < fixed, places, shifted)]].set(jnp.asarray(lengths, jnp.int32))

    lengths = jnp.where(number % 4 == 0, named(crowded, number // 4), named(usual, number - number // 4 - 1))
    mixed = jax.random.permutation(jax.random.fold_in(own, 3), amount)
    giver, taker = mixed[0:amount // 2 * 2:2], mixed[1:amount // 2 * 2:2]
    slack = jnp.minimum(lengths[giver] - 1, reach - lengths[taker]) // 2
    slack = jnp.where((giver == sequence[0]) | (taker == sequence[0]) | (lengths[taker] == 0), 0, jnp.maximum(slack, 0))
    shifted = jax.random.randint(jax.random.fold_in(own, 4), (amount // 2,), 0, 1 << 20) % (slack + 1)
    lengths = lengths.at[giver].add(-shifted).at[taker].add(shifted)
    items = jnp.searchsorted(jnp.cumsum(lengths), jnp.arange(rows * top), side="right").astype(jnp.int32)
    listing = items.reshape(top, rows).T
    listing = listing[jax.random.permutation(jax.random.fold_in(own, 1), rows)]
    turn = jax.random.randint(jax.random.fold_in(own, 2), (rows, 1), 0, top)
    return jnp.take_along_axis(listing, (jnp.arange(top)[None, :] + turn) % top, axis=1)


def load_shares(amount, total, reach, skew, full):
    portions = [(1 << 20) // math.isqrt(rank ** skew) + 1 for rank in range(1, amount + 1)]
    largest = reach if full else min(reach, max(-(-total // amount), total * portions[0] // sum(portions)))
    least = 1 if total - largest >= amount - 1 else 0
    given, rest = [largest] + [least] * (amount - 1), total - largest - least * (amount - 1)
    while rest > 0:
        movable = [i for i in range(1, amount) if given[i] < largest] or [i for i in range(1, amount) if given[i] < reach]
        pool, remaining = sum([portions[i] for i in movable]), rest
        for i in movable:
            more = min(reach - given[i], max(1, remaining * portions[i] // pool), rest)
            given[i] = given[i] + more
            rest = rest - more
    return np.array(given)


def normal_values(rng, extent, width, limit, pieces=(), kind=jnp.bfloat16):
    factor_of = steps_of(rng, extent, pieces, -0.22, 0.18) if pieces else 1.0
    array = jax.random.normal(rng, extent, jnp.float32) * width * factor_of
    return jnp.minimum(jnp.maximum(array, -limit), limit).astype(kind)


def setup_inputs(seed: int = 0) -> dict:
    key_list = jax.random.split(jax.random.key(seed), 8)
    frames_in = normal_values(key_list[0], (UTTS, FRAMES, D), 1.0, 6.0, ((0, 32), (1, 16)))
    conv_kernel = normal_values(key_list[1], (KSIZE, D), KSIZE ** -0.5, 1.0)
    norm_gain = jnp.clip(1.0 + 0.18 * jax.random.normal(key_list[2], (D,), jnp.float32), 0.099609375, 1.8984375).astype(jnp.bfloat16)
    router = normal_values(key_list[3], (D, EXPERTS), D ** -0.5, 0.15625)
    w_in = normal_values(key_list[4], (EXPERTS, FF, D), D ** -0.5, 0.15625, ((0, 32), (1, 16)))
    w_out = normal_values(key_list[5], (EXPERTS, FF, D), FF ** -0.5, 0.109375, ((0, 32), (1, 16)))
    routes_keys = jax.random.split(jax.random.fold_in(key_list[6], 1), UTTS * FRAMES // TOK_DEV)
    routes_turns = jax.random.permutation(jax.random.fold_in(key_list[6], 3), UTTS * FRAMES // TOK_DEV)
    routes = jax.vmap(lambda own, number: shared_out(jax.random.fold_in(key_list[6], 2), own, number, TOK_DEV, EXPERTS, TOP, CAP, 2))(routes_keys, routes_turns).reshape((UTTS, FRAMES, TOP))
    return {"frames_in": frames_in, "conv_kernel": conv_kernel, "norm_gain": norm_gain, "router": router, "w_in": w_in, "w_out": w_out, "routes": routes}


def reference(frames_in, conv_kernel, norm_gain, router, w_in, w_out, routes):
    margin = (KSIZE - 1) // 2
    frames_f = frames_in.astype(jnp.float32)
    padded = jnp.pad(frames_f, ((0, 0), (margin, margin), (0, 0)))
    convolved = jnp.zeros_like(frames_f)
    for offset in range(KSIZE):
        convolved = convolved + conv_kernel[offset].astype(jnp.float32) * padded[:, offset:offset + FRAMES]
    residual = frames_f + jax.nn.silu(convolved)
    scale_rms = lax.rsqrt(lax.optimization_barrier(jnp.mean(residual * residual, axis=-1, keepdims=True)) + 1e-06)
    normed = (residual * scale_rms * norm_gain.astype(jnp.float32)).astype(jnp.bfloat16)
    logits = jnp.einsum('utd,de->ute', normed.astype(jnp.float32), router.astype(jnp.float32))
    onehot = (routes[..., None] == jnp.arange(EXPERTS, dtype=jnp.int32)).astype(jnp.float32)
    gating = jax.nn.sigmoid(lax.optimization_barrier(jnp.sum(onehot * logits[:, :, None, :], axis=-1)))
    pair_count = TOK_DEV * TOP
    block_hot = onehot.reshape(UTTS, N_DP, pair_count, EXPERTS)
    earlier = jnp.cumsum(block_hot, axis=2) - block_hot
    slot_float = lax.optimization_barrier(jnp.sum(earlier * block_hot, axis=-1))
    slot_of = slot_float.astype(jnp.int32)
    slot_hot = (slot_of[..., None] == jnp.arange(CAP, dtype=jnp.int32)).astype(jnp.float32)
    normed_rep = jnp.broadcast_to(normed[:, :, None, :], (UTTS, FRAMES, TOP, D)).reshape(UTTS, N_DP, pair_count, D).astype(jnp.float32)

    def one_expert(packed):
        expert_idx, first_w, second_w = packed
        column = (jnp.arange(EXPERTS, dtype=jnp.int32) == expert_idx).astype(jnp.float32)
        mine = lax.optimization_barrier(jnp.sum(block_hot * column, axis=-1))
        chooser = mine[..., None] * slot_hot
        normed_rows = jnp.einsum('uvrc,uvrd->uvcd', chooser, normed_rep).astype(jnp.bfloat16).reshape(-1, D)
        preact = jnp.dot(normed_rows, first_w.T, preferred_element_type=jnp.float32)
        hidden = jax.nn.silu(preact).astype(jnp.bfloat16)
        expert_out = jnp.dot(hidden, second_w, preferred_element_type=jnp.float32).astype(jnp.bfloat16)
        return expert_out.reshape(UTTS, N_DP, CAP, D)
    expert_outs = lax.map(one_expert, (jnp.arange(EXPERTS, dtype=jnp.int32), w_in, w_out))
    route_flat = routes.reshape(UTTS, N_DP, pair_count).astype(jnp.int32)
    utt_idx = jnp.arange(UTTS, dtype=jnp.int32)[:, None, None]
    dev_idx = jnp.arange(N_DP, dtype=jnp.int32)[None, :, None]
    picked = expert_outs[route_flat, utt_idx, dev_idx, slot_of]
    picked = picked.astype(jnp.float32).reshape(UTTS, FRAMES, TOP, D)
    combined = (residual + lax.optimization_barrier(jnp.sum(gating[..., None] * picked, axis=2))).astype(jnp.bfloat16)
    return combined
```

```python
import functools

import jax
import jax.numpy as jnp
from jax import lax
from jax.experimental import pallas as pl
from jax.experimental.pallas import tpu as pltpu
from jax.sharding import PartitionSpec as P

MAIN = 8
LANES = 128
WIDE = 256
HALO = 16
bf16, f32, i32 = jnp.bfloat16, jnp.float32, jnp.int32
TRANSPOSED = (((1,), (1,)), ((), ()))


def dot(a, b):
    return jnp.dot(a, b, preferred_element_type=f32)


def iota(shape, dim):
    return lax.broadcasted_iota(i32, shape, dim)


def call(kernel, outs, args, flops, scratch=(), aliases={}, limit=48 << 20):
    moved = sum(x.size * x.dtype.itemsize for x in (*args, *outs))
    return pl.pallas_call(
        kernel,
        out_shape=outs,
        in_specs=[pl.BlockSpec(memory_space=pltpu.VMEM)] * len(args),
        out_specs=tuple(pl.BlockSpec(memory_space=pltpu.VMEM) for _ in outs),
        scratch_shapes=scratch,
        input_output_aliases=aliases,
        compiler_params=pltpu.CompilerParams(vmem_limit_bytes=limit),
        cost_estimate=pl.CostEstimate(flops=flops, bytes_accessed=moved, transcendentals=0),
    )(*args)


def shape(dims, dtype):
    return jax.ShapeDtypeStruct(dims, dtype)


def front_kernel(taps, x_ref, low_ref, high_ref, kernel_ref, gain_ref, router_ref, routes_ref,
                 sent_ref, res_ref, high_w_ref, low_w_ref, high_x_ref, low_x_ref, padded, kernels):
    tok, features = x_ref.shape
    tiles = features // LANES
    skip = HALO - (taps - 1) // 2
    for c in range(tiles):
        cols = slice(c * LANES, (c + 1) * LANES)
        padded[c, :HALO] = low_ref[:, cols].astype(f32)
        padded[c, HALO : HALO + tok] = x_ref[:, cols].astype(f32)
        padded[c, HALO + tok :] = high_ref[:, cols].astype(f32)
        kernels[c, :taps] = kernel_ref[:, cols].astype(f32)

    def column(c, squares):
        acc = jnp.zeros((tok, LANES), f32)
        for j in range(taps):
            acc = acc + kernels[c, pl.ds(j, 1), :] * padded[c, pl.ds(j + skip, tok), :]
        res = padded[c, pl.ds(HALO, tok), :] + acc / (1.0 + jnp.exp(-acc))
        res_ref[:, pl.ds(pl.multiple_of(c * LANES, LANES), LANES)] = res
        return squares + res * res

    squares = lax.fori_loop(0, tiles, column, jnp.zeros((tok, LANES), f32))
    mean = jnp.sum(squares, axis=-1, keepdims=True) / features
    scale = lax.rsqrt(mean + 1e-06)
    normed = (res_ref[...] * scale * gain_ref[...].astype(f32)).astype(bf16)

    experts = router_ref.shape[0]
    rows = experts * MAIN
    expert_of = iota((experts, tok), 0)
    hots = [(expert_of == routes_ref[k : k + 1, :]).astype(f32) for k in range(2)]
    before = (iota((tok, tok), 0) < iota((tok, tok), 1)).astype(bf16)
    counts = dot((hots[0] + hots[1]).astype(bf16), before)
    logits = lax.dot_general(router_ref[...], normed, TRANSPOSED, preferred_element_type=f32)
    place = iota((rows, tok), 0)
    main = jnp.zeros((rows, tok), f32)
    extra = jnp.zeros((rows, tok), f32)
    main_w = jnp.zeros((rows, tok), f32)
    extra_w = jnp.zeros((rows, tok), f32)
    for k in range(2):
        slot = jnp.sum(counts * hots[k], axis=0, keepdims=True).astype(i32)
        logit = jnp.sum(logits * hots[k], axis=0, keepdims=True)
        gate = 1.0 / (1.0 + jnp.exp(-logit))
        expert = routes_ref[k : k + 1, :]
        inside = slot < MAIN
        first = jnp.where(inside, expert * MAIN + slot, -1)
        hit = place == first
        main = main + hit.astype(f32)
        main_w = main_w + jnp.where(hit, gate, 0.0)
        last = jnp.where(inside, -1, expert)
        hit = lax.shift_right_arithmetic(place, 3) == last
        extra = extra + hit.astype(f32)
        extra_w = extra_w + jnp.where(hit, gate, 0.0)
    sent_ref[:, :features] = dot(main.astype(bf16), normed).astype(bf16)
    pieces = jnp.zeros((rows, WIDE), f32)
    piece_of = jnp.bitwise_and(place, MAIN - 1)
    for j in range(features // WIDE):
        chosen = jnp.where(piece_of == j, extra, 0.0).astype(bf16)
        pieces = pieces + dot(chosen, normed[:, j * WIDE : (j + 1) * WIDE])
    sent_ref[:, features:] = pieces.astype(bf16)
    for weights, high, low in ((main_w, high_w_ref, low_w_ref), (extra_w, high_x_ref, low_x_ref)):
        turned = weights.T
        coarse = turned.astype(bf16)
        high[...] = coarse
        low[...] = (turned - coarse.astype(f32)).astype(bf16)


def front(x, low, high, kernel, gain, router, routes):
    tok, features = x.shape
    taps = kernel.shape[0]
    rows = router.shape[0] * MAIN
    outs = (
        shape((rows, features + WIDE), bf16),
        shape((tok, features), f32),
        *(shape((tok, rows), bf16) for _ in range(4)),
    )
    tiles = features // LANES
    return call(
        functools.partial(front_kernel, taps),
        outs,
        (x, low, high, kernel, gain, router, routes),
        flops=20_000_000_000,
        scratch=[pltpu.VMEM((tiles, tok + 2 * HALO, LANES), f32), pltpu.VMEM((tiles, 32, LANES), f32)],
    )


def ffn(rows, blocks):
    first = jnp.concatenate([b[0] for b in blocks], axis=0)
    second = jnp.concatenate([b[1] for b in blocks], axis=0)
    preact = lax.dot_general(rows, first, TRANSPOSED, preferred_element_type=f32)
    hidden = (preact / (1.0 + jnp.exp(-preact))).astype(bf16)
    return hidden, second


def unpacked(packed_ref, rows_ref, base, features):
    count = packed_ref.shape[0]
    experts = count // MAIN
    rows_ref[base : base + count] = packed_ref[:, :features]
    pieces = packed_ref[:, features:]
    for j in range(features // WIDE):
        pick = (iota((experts, count), 1) == iota((experts, count), 0) * MAIN + j).astype(bf16)
        rows_ref[base + count : base + count + experts, j * WIDE : (j + 1) * WIDE] = dot(pick, pieces).astype(bf16)


def accumulate(hidden, second, out_ref, old_ref=None):
    for n in range(0, second.shape[1], 512):
        part = dot(hidden, second[:, n : n + 512])
        out_ref[:, n : n + 512] = part if old_ref is None else old_ref[:, n : n + 512] + part


def begin_kernel(mine_ref, other_ref, *refs):
    *blocks, rows_ref, total_ref = refs
    features = rows_ref.shape[1]
    unpacked(mine_ref, rows_ref, 0, features)
    unpacked(other_ref, rows_ref, rows_ref.shape[0] // 2, features)
    hidden, second = ffn(rows_ref[...], blocks)
    accumulate(hidden, second, total_ref)


def more_kernel(rows_ref, old_ref, *refs):
    *blocks, total_ref = refs
    hidden, second = ffn(rows_ref[...], blocks)
    accumulate(hidden, second, total_ref, old_ref)


def end_kernel(rows_ref, old_ref, *refs):
    *blocks, mine_ref, other_ref = refs
    hidden, second = ffn(rows_ref[...], blocks)
    half = rows_ref.shape[0] // 2
    for n in range(0, second.shape[1], 512):
        part = old_ref[:, n : n + 512] + dot(hidden, second[:, n : n + 512])
        mine_ref[:, n : n + 512] = part[:half]
        other_ref[:, n : n + 512] = part[half:].astype(bf16)


def pack_kernel(mine_ref, other_ref, packed_ref):
    count, features = packed_ref.shape[0], mine_ref.shape[1]
    experts = count // MAIN
    summed = (mine_ref[...] + other_ref[...].astype(f32)).astype(bf16)
    packed_ref[:, :features] = summed[:count]
    extra = summed[count:]
    pieces = jnp.zeros((count, WIDE), f32)
    for j in range(features // WIDE):
        place = (iota((count, experts), 0) == iota((count, experts), 1) * MAIN + j).astype(bf16)
        pieces = pieces + dot(place, extra[:, j * WIDE : (j + 1) * WIDE])
    packed_ref[:, features:] = pieces.astype(bf16)


def combine_kernel(back_ref, res_ref, high_w_ref, low_w_ref, high_x_ref, low_x_ref, out_ref):
    tok, features = res_ref.shape
    count = back_ref.shape[0]
    pieces = back_ref[:, features:]
    piece_of = jnp.bitwise_and(iota((tok, count), 1), MAIN - 1)
    for j in range(features // WIDE):
        cols = slice(j * WIDE, (j + 1) * WIDE)
        here = piece_of == j
        back = back_ref[:, cols]
        pulled = dot(high_w_ref[...], back) + dot(low_w_ref[...], back)
        for ref in (high_x_ref, low_x_ref):
            weights = jnp.where(here, ref[...].astype(f32), 0.0).astype(bf16)
            pulled = pulled + dot(weights, pieces)
        out_ref[:, cols] = (res_ref[:, cols] + pulled).astype(bf16)


def shards(frames_in, conv_kernel, norm_gain, router, w_in, w_out, routes):
    tok, features = frames_in.shape[1:]
    experts = router.shape[1]
    dp = lax.axis_size("dp")
    chips = dp // 2
    up = [(i, (i + 2) % dp) for i in range(dp)]
    down = [(i, (i - 2) % dp) for i in range(dp)]
    sibling = [(i, i ^ 1) for i in range(dp)]
    frames = frames_in[0]

    low = lax.ppermute(frames[tok - HALO :], "dp", [(i, i + 1) for i in range(dp - 1)])
    high = lax.ppermute(frames[:HALO], "dp", [(i + 1, i) for i in range(dp - 1)])

    own = jnp.concatenate([w_in, w_out], axis=0)
    a1, b1 = lax.ppermute(own, "dp", up), lax.ppermute(own, "dp", down)
    sent, residual, *weights = front(
        frames, low, high, conv_kernel, norm_gain[None], router.T, routes[0].T
    )
    sent, a1, b1 = lax.optimization_barrier((sent, a1, b1))
    a2, b2 = lax.ppermute(a1, "dp", up), lax.ppermute(b1, "dp", down)
    a3, b3 = lax.ppermute(a2, "dp", up), lax.ppermute(b2, "dp", down)
    half = own.shape[1] // 2
    a4, b4 = lax.ppermute(a3[:, :half], "dp", up), lax.ppermute(b3[:, half:], "dp", down)
    assert chips == 8

    def exchange(v):
        parts = v.reshape(experts, MAIN, v.shape[1])
        out = lax.all_to_all(parts, "expert", split_axis=0, concat_axis=0, tiled=True)
        return out.reshape(v.shape)

    mine = exchange(sent)
    other = lax.ppermute(mine, "dp", sibling)
    count = experts * (MAIN + 1)
    flops = lambda units: 2 * 2 * 2 * count * units * features
    units = own.shape[1]
    rows, total = call(
        begin_kernel,
        (shape((2 * count, features), bf16), shape((2 * count, features), f32)),
        (mine, other, own, a1, b1, a2, b2),
        flops(5 * units),
    )
    (total,) = call(
        more_kernel, (shape(total.shape, f32),), (rows, total, a3, b3), flops(2 * units), aliases={1: 0}
    )
    kept, gone = call(
        end_kernel,
        (shape((count, features), f32), shape((count, features), bf16)),
        (rows, total, a4, b4),
        flops(units),
    )
    came = lax.ppermute(gone, "dp", sibling)
    (packed,) = call(pack_kernel, (shape(sent.shape, bf16),), (kept, came), 10_000_000)
    back = exchange(packed)
    (out,) = call(combine_kernel, (shape((tok, features), bf16),), (back, residual, *weights), 10_000_000)
    return out[None]


def solution(mesh):
    rows = P("expert", "dp", None)
    return jax.shard_map(
        shards,
        mesh=mesh,
        in_specs=(rows, P(), P(), P(), rows, rows, rows),
        out_specs=rows,
        check_vma=False,
    )
```

```python
import functools

import jax
import jax.numpy as jnp
from jax import lax
from jax.experimental import pallas as pl
from jax.experimental.pallas import tpu as pltpu
from jax.sharding import PartitionSpec as P

MAIN = 8
LANES = 128
WIDE = 256
HALO = 16
bf16, f32, i32 = jnp.bfloat16, jnp.float32, jnp.int32
TRANSPOSED = (((1,), (1,)), ((), ()))


def dot(a, b):
    return jnp.dot(a, b, preferred_element_type=f32)


def iota(shape, dim):
    return lax.broadcasted_iota(i32, shape, dim)


def call(kernel, outs, args, flops, scratch=(), aliases={}, limit=20 << 20):
    moved = sum(x.size * x.dtype.itemsize for x in (*args, *outs))
    return pl.pallas_call(
        kernel,
        out_shape=outs,
        in_specs=[pl.BlockSpec(memory_space=pltpu.VMEM)] * len(args),
        out_specs=tuple(pl.BlockSpec(memory_space=pltpu.VMEM) for _ in outs),
        scratch_shapes=scratch,
        input_output_aliases=aliases,
        compiler_params=pltpu.CompilerParams(vmem_limit_bytes=limit),
        cost_estimate=pl.CostEstimate(flops=flops, bytes_accessed=moved, transcendentals=0),
    )(*args)


def shape(dims, dtype):
    return jax.ShapeDtypeStruct(dims, dtype)


def front_kernel(taps, x_ref, low_ref, high_ref, kernel_ref, gain_ref, router_ref, routes_ref,
                 sent_ref, res_ref, high_w_ref, low_w_ref, high_x_ref, low_x_ref, padded, kernels):
    tok, features = x_ref.shape
    tiles = features // LANES
    skip = HALO - (taps - 1) // 2
    for c in range(tiles):
        cols = slice(c * LANES, (c + 1) * LANES)
        padded[c, :HALO] = low_ref[:, cols].astype(f32)
        padded[c, HALO : HALO + tok] = x_ref[:, cols].astype(f32)
        padded[c, HALO + tok :] = high_ref[:, cols].astype(f32)
        kernels[c, :taps] = kernel_ref[:, cols].astype(f32)

    def column(c, squares):
        acc = jnp.zeros((tok, LANES), f32)
        for j in range(taps):
            acc = acc + kernels[c, pl.ds(j, 1), :] * padded[c, pl.ds(j + skip, tok), :]
        res = padded[c, pl.ds(HALO, tok), :] + acc / (1.0 + jnp.exp(-acc))
        res_ref[:, pl.ds(pl.multiple_of(c * LANES, LANES), LANES)] = res
        return squares + res * res

    squares = lax.fori_loop(0, tiles, column, jnp.zeros((tok, LANES), f32))
    mean = jnp.sum(squares, axis=-1, keepdims=True) / features
    scale = lax.rsqrt(mean + 1e-06)
    normed = (res_ref[...] * scale * gain_ref[...].astype(f32)).astype(bf16)

    experts = router_ref.shape[0]
    rows = experts * MAIN
    expert_of = iota((experts, tok), 0)
    hots = [(expert_of == routes_ref[k : k + 1, :]).astype(f32) for k in range(2)]
    before = (iota((tok, tok), 0) < iota((tok, tok), 1)).astype(bf16)
    counts = dot((hots[0] + hots[1]).astype(bf16), before)
    logits = lax.dot_general(router_ref[...], normed, TRANSPOSED, preferred_element_type=f32)
    place = iota((rows, tok), 0)
    main = jnp.zeros((rows, tok), f32)
    extra = jnp.zeros((rows, tok), f32)
    main_w = jnp.zeros((rows, tok), f32)
    extra_w = jnp.zeros((rows, tok), f32)
    for k in range(2):
        slot = jnp.sum(counts * hots[k], axis=0, keepdims=True).astype(i32)
        logit = jnp.sum(logits * hots[k], axis=0, keepdims=True)
        gate = 1.0 / (1.0 + jnp.exp(-logit))
        expert = routes_ref[k : k + 1, :]
        inside = slot < MAIN
        first = jnp.where(inside, expert * MAIN + slot, -1)
        hit = place == first
        main = main + hit.astype(f32)
        main_w = main_w + jnp.where(hit, gate, 0.0)
        last = jnp.where(inside, -1, expert)
        hit = lax.shift_right_arithmetic(place, 3) == last
        extra = extra + hit.astype(f32)
        extra_w = extra_w + jnp.where(hit, gate, 0.0)
    sent_ref[:, :features] = dot(main.astype(bf16), normed).astype(bf16)
    pieces = jnp.zeros((rows, WIDE), f32)
    piece_of = jnp.bitwise_and(place, MAIN - 1)
    for j in range(features // WIDE):
        chosen = jnp.where(piece_of == j, extra, 0.0).astype(bf16)
        pieces = pieces + dot(chosen, normed[:, j * WIDE : (j + 1) * WIDE])
    sent_ref[:, features:] = pieces.astype(bf16)
    for weights, high, low in ((main_w, high_w_ref, low_w_ref), (extra_w, high_x_ref, low_x_ref)):
        turned = weights.T
        coarse = turned.astype(bf16)
        high[...] = coarse
        low[...] = (turned - coarse.astype(f32)).astype(bf16)


def front(x, low, high, kernel, gain, router, routes):
    tok, features = x.shape
    taps = kernel.shape[0]
    rows = router.shape[0] * MAIN
    outs = (
        shape((rows, features + WIDE), bf16),
        shape((tok, features), f32),
        *(shape((tok, rows), bf16) for _ in range(4)),
    )
    tiles = features // LANES
    return call(
        functools.partial(front_kernel, taps),
        outs,
        (x, low, high, kernel, gain, router, routes),
        flops=20_000_000_000,
        scratch=[pltpu.VMEM((tiles, tok + 2 * HALO, LANES), f32), pltpu.VMEM((tiles, 32, LANES), f32)],
    )


def ffn(rows, blocks):
    whole = [b for b in blocks if len(b.shape) == 3]
    split = [b for b in blocks if len(b.shape) == 2]
    first = jnp.concatenate([b[0] for b in whole] + [b[...] for b in split[::2]], axis=0)
    second = jnp.concatenate([b[1] for b in whole] + [b[...] for b in split[1::2]], axis=0)
    preact = lax.dot_general(rows, first, TRANSPOSED, preferred_element_type=f32)
    hidden = (preact / (1.0 + jnp.exp(-preact))).astype(bf16)
    return hidden, second


def unpacked(packed_ref, rows_ref, base, features):
    count = packed_ref.shape[0]
    experts = count // MAIN
    rows_ref[base : base + count] = packed_ref[:, :features]
    pieces = packed_ref[:, features:]
    for j in range(features // WIDE):
        pick = (iota((experts, count), 1) == iota((experts, count), 0) * MAIN + j).astype(bf16)
        rows_ref[base + count : base + count + experts, j * WIDE : (j + 1) * WIDE] = dot(pick, pieces).astype(bf16)


def accumulate(hidden, second, out_ref, old_ref=None):
    for n in range(0, second.shape[1], 512):
        part = dot(hidden, second[:, n : n + 512])
        out_ref[:, n : n + 512] = part if old_ref is None else old_ref[:, n : n + 512] + part


def begin_kernel(mine_ref, other_ref, *refs):
    *blocks, rows_ref, total_ref = refs
    features = rows_ref.shape[1]
    unpacked(mine_ref, rows_ref, 0, features)
    unpacked(other_ref, rows_ref, rows_ref.shape[0] // 2, features)
    hidden, second = ffn(rows_ref[...], blocks)
    accumulate(hidden, second, total_ref)


def more_kernel(rows_ref, old_ref, *refs):
    *blocks, total_ref = refs
    hidden, second = ffn(rows_ref[...], blocks)
    accumulate(hidden, second, total_ref, old_ref)


def end_kernel(rows_ref, old_ref, *refs):
    *blocks, mine_ref, other_ref = refs
    hidden, second = ffn(rows_ref[...], blocks)
    half = rows_ref.shape[0] // 2
    for n in range(0, second.shape[1], 512):
        part = old_ref[:, n : n + 512] + dot(hidden, second[:, n : n + 512])
        mine_ref[:, n : n + 512] = part[:half]
        other_ref[:, n : n + 512] = part[half:].astype(bf16)


def pack_kernel(mine_ref, other_ref, packed_ref):
    count, features = packed_ref.shape[0], mine_ref.shape[1]
    experts = count // MAIN
    summed = (mine_ref[...] + other_ref[...].astype(f32)).astype(bf16)
    packed_ref[:, :features] = summed[:count]
    extra = summed[count:]
    pieces = jnp.zeros((count, WIDE), f32)
    for j in range(features // WIDE):
        place = (iota((count, experts), 0) == iota((count, experts), 1) * MAIN + j).astype(bf16)
        pieces = pieces + dot(place, extra[:, j * WIDE : (j + 1) * WIDE])
    packed_ref[:, features:] = pieces.astype(bf16)


def combine_kernel(back_ref, res_ref, high_w_ref, low_w_ref, high_x_ref, low_x_ref, out_ref):
    tok, features = res_ref.shape
    count = back_ref.shape[0]
    pieces = back_ref[:, features:]
    piece_of = jnp.bitwise_and(iota((tok, count), 1), MAIN - 1)
    for j in range(features // WIDE):
        cols = slice(j * WIDE, (j + 1) * WIDE)
        here = piece_of == j
        back = back_ref[:, cols]
        pulled = dot(high_w_ref[...], back) + dot(low_w_ref[...], back)
        for ref in (high_x_ref, low_x_ref):
            weights = jnp.where(here, ref[...].astype(f32), 0.0).astype(bf16)
            pulled = pulled + dot(weights, pieces)
        out_ref[:, cols] = (res_ref[:, cols] + pulled).astype(bf16)


def shards(frames_in, conv_kernel, norm_gain, router, w_in, w_out, routes):
    tok, features = frames_in.shape[1:]
    experts = router.shape[1]
    dp = lax.axis_size("dp")
    chips = dp // 2
    up = [(i, (i + 2) % dp) for i in range(dp)]
    down = [(i, (i - 2) % dp) for i in range(dp)]
    sibling = [(i, i ^ 1) for i in range(dp)]
    frames = frames_in[0]

    low = lax.ppermute(frames[tok - HALO :], "dp", [(i, i + 1) for i in range(dp - 1)])
    high = lax.ppermute(frames[:HALO], "dp", [(i + 1, i) for i in range(dp - 1)])

    units = w_in.shape[1]
    own = jnp.concatenate([w_in, w_out], axis=0)
    a1, b1 = lax.ppermute(own, "dp", up), lax.ppermute(own, "dp", down)

    def step(ups, downs):
        moved = [(lax.ppermute(a, "dp", up), lax.ppermute(b, "dp", down)) for a, b in zip(ups, downs)]
        return [m[0] for m in moved], [m[1] for m in moved]

    a2, b2 = step([a1[0], a1[1]], [b1[0], b1[1]])
    a3, b3 = step(a2, b2)
    sent, residual, *weights = front(
        frames, low, high, conv_kernel, norm_gain[None], router.T, routes[0].T
    )
    assert chips == 8

    def exchange(v):
        parts = v.reshape(experts, MAIN, v.shape[1])
        out = lax.all_to_all(parts, "expert", split_axis=0, concat_axis=0, tiled=True)
        return out.reshape(v.shape)

    mine = exchange(sent)
    other = lax.ppermute(mine, "dp", sibling)
    count = experts * (MAIN + 1)
    flops = lambda units: 2 * 2 * 2 * count * units * features
    rows, total = call(
        begin_kernel,
        (shape((2 * count, features), bf16), shape((2 * count, features), f32)),
        (mine, other, own, a1, b1, *a2, *b2),
        flops(5 * units),
    )
    total, a3[0], b3[0] = lax.optimization_barrier((total, a3[0], b3[0]))
    half = units // 2
    a4, b4 = step([a[:half] for a in a3], [b[half:] for b in b3])
    (total,) = call(
        more_kernel, (shape(total.shape, f32),), (rows, total, *a3, *b3), flops(2 * units), aliases={1: 0}
    )
    kept, gone = call(
        end_kernel,
        (shape((count, features), f32), shape((count, features), bf16)),
        (rows, total, *a4, *b4),
        flops(units),
    )
    came = lax.ppermute(gone, "dp", sibling)
    (packed,) = call(pack_kernel, (shape(sent.shape, bf16),), (kept, came), 10_000_000)
    back = exchange(packed)
    (out,) = call(combine_kernel, (shape((tok, features), bf16),), (back, residual, *weights), 10_000_000)
    return out[None]


def solution(mesh):
    rows = P("expert", "dp", None)
    return jax.shard_map(
        shards,
        mesh=mesh,
        in_specs=(rows, P(), P(), P(), rows, rows, rows),
        out_specs=rows,
        check_vma=False,
    )
```

```python
import functools

import jax
import jax.numpy as jnp
from jax import lax
from jax.experimental import pallas as pl
from jax.experimental.pallas import tpu as pltpu
from jax.sharding import PartitionSpec as P

MAIN = 8
LANES = 128
WIDE = 256
HALO = 16
bf16, f32, i32 = jnp.bfloat16, jnp.float32, jnp.int32
TRANSPOSED = (((1,), (1,)), ((), ()))


def dot(a, b):
    return jnp.dot(a, b, preferred_element_type=f32)


def iota(shape, dim):
    return lax.broadcasted_iota(i32, shape, dim)


def call(kernel, outs, args, flops, scratch=(), aliases={}, limit=20 << 20):
    moved = sum(x.size * x.dtype.itemsize for x in (*args, *outs))
    return pl.pallas_call(
        kernel,
        out_shape=outs,
        in_specs=[pl.BlockSpec(memory_space=pltpu.VMEM)] * len(args),
        out_specs=tuple(pl.BlockSpec(memory_space=pltpu.VMEM) for _ in outs),
        scratch_shapes=scratch,
        input_output_aliases=aliases,
        compiler_params=pltpu.CompilerParams(vmem_limit_bytes=limit),
        cost_estimate=pl.CostEstimate(flops=flops, bytes_accessed=moved, transcendentals=0),
    )(*args)


def shape(dims, dtype):
    return jax.ShapeDtypeStruct(dims, dtype)


def front_kernel(taps, x_ref, low_ref, high_ref, kernel_ref, gain_ref, router_ref, routes_ref,
                 sent_ref, res_ref, high_w_ref, low_w_ref, high_x_ref, low_x_ref, padded, kernels):
    tok, features = x_ref.shape
    tiles = features // LANES
    skip = HALO - (taps - 1) // 2
    for c in range(tiles):
        cols = slice(c * LANES, (c + 1) * LANES)
        padded[c, :HALO] = low_ref[:, cols].astype(f32)
        padded[c, HALO : HALO + tok] = x_ref[:, cols].astype(f32)
        padded[c, HALO + tok :] = high_ref[:, cols].astype(f32)
        kernels[c, :taps] = kernel_ref[:, cols].astype(f32)

    def column(c, squares):
        acc = jnp.zeros((tok, LANES), f32)
        for j in range(taps):
            acc = acc + kernels[c, pl.ds(j, 1), :] * padded[c, pl.ds(j + skip, tok), :]
        res = padded[c, pl.ds(HALO, tok), :] + acc / (1.0 + jnp.exp(-acc))
        res_ref[:, pl.ds(pl.multiple_of(c * LANES, LANES), LANES)] = res
        return squares + res * res

    squares = lax.fori_loop(0, tiles, column, jnp.zeros((tok, LANES), f32))
    mean = jnp.sum(squares, axis=-1, keepdims=True) / features
    scale = lax.rsqrt(mean + 1e-06)
    normed = (res_ref[...] * scale * gain_ref[...].astype(f32)).astype(bf16)

    experts = router_ref.shape[0]
    rows = experts * MAIN
    expert_of = iota((experts, tok), 0)
    hots = [(expert_of == routes_ref[k : k + 1, :]).astype(f32) for k in range(2)]
    before = (iota((tok, tok), 0) < iota((tok, tok), 1)).astype(bf16)
    counts = dot((hots[0] + hots[1]).astype(bf16), before)
    logits = lax.dot_general(router_ref[...], normed, TRANSPOSED, preferred_element_type=f32)
    place = iota((rows, tok), 0)
    main = jnp.zeros((rows, tok), f32)
    extra = jnp.zeros((rows, tok), f32)
    main_w = jnp.zeros((rows, tok), f32)
    extra_w = jnp.zeros((rows, tok), f32)
    for k in range(2):
        slot = jnp.sum(counts * hots[k], axis=0, keepdims=True).astype(i32)
        logit = jnp.sum(logits * hots[k], axis=0, keepdims=True)
        gate = 1.0 / (1.0 + jnp.exp(-logit))
        expert = routes_ref[k : k + 1, :]
        inside = slot < MAIN
        first = jnp.where(inside, expert * MAIN + slot, -1)
        hit = place == first
        main = main + hit.astype(f32)
        main_w = main_w + jnp.where(hit, gate, 0.0)
        last = jnp.where(inside, -1, expert)
        hit = lax.shift_right_arithmetic(place, 3) == last
        extra = extra + hit.astype(f32)
        extra_w = extra_w + jnp.where(hit, gate, 0.0)
    sent_ref[:, :features] = dot(main.astype(bf16), normed).astype(bf16)
    pieces = jnp.zeros((rows, WIDE), f32)
    piece_of = jnp.bitwise_and(place, MAIN - 1)
    for j in range(features // WIDE):
        chosen = jnp.where(piece_of == j, extra, 0.0).astype(bf16)
        pieces = pieces + dot(chosen, normed[:, j * WIDE : (j + 1) * WIDE])
    sent_ref[:, features:] = pieces.astype(bf16)
    for weights, high, low in ((main_w, high_w_ref, low_w_ref), (extra_w, high_x_ref, low_x_ref)):
        turned = weights.T
        coarse = turned.astype(bf16)
        high[...] = coarse
        low[...] = (turned - coarse.astype(f32)).astype(bf16)


def front(x, low, high, kernel, gain, router, routes):
    tok, features = x.shape
    taps = kernel.shape[0]
    rows = router.shape[0] * MAIN
    outs = (
        shape((rows, features + WIDE), bf16),
        shape((tok, features), f32),
        *(shape((tok, rows), bf16) for _ in range(4)),
    )
    tiles = features // LANES
    return call(
        functools.partial(front_kernel, taps),
        outs,
        (x, low, high, kernel, gain, router, routes),
        flops=20_000_000_000,
        scratch=[pltpu.VMEM((tiles, tok + 2 * HALO, LANES), f32), pltpu.VMEM((tiles, 32, LANES), f32)],
    )


def ffn(rows, blocks):
    whole = [b for b in blocks if len(b.shape) == 3]
    split = [b for b in blocks if len(b.shape) == 2]
    first = jnp.concatenate([b[0] for b in whole] + [b[...] for b in split[::2]], axis=0)
    second = jnp.concatenate([b[1] for b in whole] + [b[...] for b in split[1::2]], axis=0)
    preact = lax.dot_general(rows, first, TRANSPOSED, preferred_element_type=f32)
    hidden = (preact / (1.0 + jnp.exp(-preact))).astype(bf16)
    return hidden, second


def unpacked(packed_ref, rows_ref, base, features):
    count = packed_ref.shape[0]
    experts = count // MAIN
    rows_ref[base : base + count] = packed_ref[:, :features]
    pieces = packed_ref[:, features:]
    for j in range(features // WIDE):
        pick = (iota((experts, count), 1) == iota((experts, count), 0) * MAIN + j).astype(bf16)
        rows_ref[base + count : base + count + experts, j * WIDE : (j + 1) * WIDE] = dot(pick, pieces).astype(bf16)


def accumulate(hidden, second, out_ref, old_ref=None):
    for n in range(0, second.shape[1], 512):
        part = dot(hidden, second[:, n : n + 512])
        out_ref[:, n : n + 512] = part if old_ref is None else old_ref[:, n : n + 512] + part


def begin_kernel(mine_ref, other_ref, *refs):
    *blocks, rows_ref, total_ref = refs
    features = rows_ref.shape[1]
    unpacked(mine_ref, rows_ref, 0, features)
    unpacked(other_ref, rows_ref, rows_ref.shape[0] // 2, features)
    hidden, second = ffn(rows_ref[...], blocks)
    accumulate(hidden, second, total_ref)


def more_kernel(rows_ref, old_ref, *refs):
    *blocks, total_ref = refs
    hidden, second = ffn(rows_ref[...], blocks)
    accumulate(hidden, second, total_ref, old_ref)


def end_kernel(own_rows, rows_ref, old_ref, *refs):
    *blocks, out_ref = refs
    half = rows_ref.shape[0] // 2
    here = slice(0, half) if own_rows else slice(half, 2 * half)
    hidden, second = ffn(rows_ref[here], blocks)
    for n in range(0, second.shape[1], 512):
        part = old_ref[here, n : n + 512] + dot(hidden, second[:, n : n + 512])
        out_ref[:, n : n + 512] = part.astype(out_ref.dtype)


def pack_kernel(mine_ref, other_ref, packed_ref):
    count, features = packed_ref.shape[0], mine_ref.shape[1]
    experts = count // MAIN
    summed = (mine_ref[...] + other_ref[...].astype(f32)).astype(bf16)
    packed_ref[:, :features] = summed[:count]
    extra = summed[count:]
    pieces = jnp.zeros((count, WIDE), f32)
    for j in range(features // WIDE):
        place = (iota((count, experts), 0) == iota((count, experts), 1) * MAIN + j).astype(bf16)
        pieces = pieces + dot(place, extra[:, j * WIDE : (j + 1) * WIDE])
    packed_ref[:, features:] = pieces.astype(bf16)


def combine_kernel(back_ref, res_ref, high_w_ref, low_w_ref, high_x_ref, low_x_ref, out_ref):
    tok, features = res_ref.shape
    count = back_ref.shape[0]
    pieces = back_ref[:, features:]
    piece_of = jnp.bitwise_and(iota((tok, count), 1), MAIN - 1)
    for j in range(features // WIDE):
        cols = slice(j * WIDE, (j + 1) * WIDE)
        here = piece_of == j
        back = back_ref[:, cols]
        pulled = dot(high_w_ref[...], back) + dot(low_w_ref[...], back)
        for ref in (high_x_ref, low_x_ref):
            weights = jnp.where(here, ref[...].astype(f32), 0.0).astype(bf16)
            pulled = pulled + dot(weights, pieces)
        out_ref[:, cols] = (res_ref[:, cols] + pulled).astype(bf16)


def shards(frames_in, conv_kernel, norm_gain, router, w_in, w_out, routes):
    tok, features = frames_in.shape[1:]
    experts = router.shape[1]
    dp = lax.axis_size("dp")
    chips = dp // 2
    up = [(i, (i + 2) % dp) for i in range(dp)]
    down = [(i, (i - 2) % dp) for i in range(dp)]
    sibling = [(i, i ^ 1) for i in range(dp)]
    frames = frames_in[0]

    low = lax.ppermute(frames[tok - HALO :], "dp", [(i, i + 1) for i in range(dp - 1)])
    high = lax.ppermute(frames[:HALO], "dp", [(i + 1, i) for i in range(dp - 1)])

    units = w_in.shape[1]
    own = jnp.concatenate([w_in, w_out], axis=0)
    a1, b1 = lax.ppermute(own, "dp", up), lax.ppermute(own, "dp", down)

    def step(ups, downs):
        moved = [(lax.ppermute(a, "dp", up), lax.ppermute(b, "dp", down)) for a, b in zip(ups, downs)]
        return [m[0] for m in moved], [m[1] for m in moved]

    a2, b2 = step([a1[0], a1[1]], [b1[0], b1[1]])
    a3, b3 = step(a2, b2)
    sent, residual, *weights = front(
        frames, low, high, conv_kernel, norm_gain[None], router.T, routes[0].T
    )
    assert chips == 8

    def exchange(v):
        parts = v.reshape(experts, MAIN, v.shape[1])
        out = lax.all_to_all(parts, "expert", split_axis=0, concat_axis=0, tiled=True)
        return out.reshape(v.shape)

    mine = exchange(sent)
    other = lax.ppermute(mine, "dp", sibling)
    count = experts * (MAIN + 1)
    flops = lambda units: 2 * 2 * 2 * count * units * features
    rows, total = call(
        begin_kernel,
        (shape((2 * count, features), bf16), shape((2 * count, features), f32)),
        (mine, other, own, a1, b1, *a2, *b2),
        flops(5 * units),
    )
    total, a3[0], b3[0] = lax.optimization_barrier((total, a3[0], b3[0]))
    half = units // 2
    a4, b4 = step([a[:half] for a in a3], [b[half:] for b in b3])
    (total,) = call(
        more_kernel, (shape(total.shape, f32),), (rows, total, *a3, *b3), flops(2 * units), aliases={1: 0}
    )
    (gone,) = call(
        functools.partial(end_kernel, False),
        (shape((count, features), bf16),),
        (rows, total, *a4, *b4),
        flops(units) // 2,
    )
    came = lax.ppermute(gone, "dp", sibling)
    (kept,) = call(
        functools.partial(end_kernel, True),
        (shape((count, features), f32),),
        (rows, total, *a4, *b4),
        flops(units) // 2,
    )
    (packed,) = call(pack_kernel, (shape(sent.shape, bf16),), (kept, came), 10_000_000)
    back = exchange(packed)
    (out,) = call(combine_kernel, (shape((tok, features), bf16),), (back, residual, *weights), 10_000_000)
    return out[None]


def solution(mesh):
    rows = P("expert", "dp", None)
    return jax.shard_map(
        shards,
        mesh=mesh,
        in_specs=(rows, P(), P(), P(), rows, rows, rows),
        out_specs=rows,
        check_vma=False,
    )
```

```python
import functools

import jax
import jax.numpy as jnp
from jax import lax
from jax.experimental import pallas as pl
from jax.experimental.pallas import tpu as pltpu
from jax.sharding import PartitionSpec as P

MAIN = 8
LANES = 128
WIDE = 256
HALO = 16
bf16, f32, i32 = jnp.bfloat16, jnp.float32, jnp.int32
TRANSPOSED = (((1,), (1,)), ((), ()))


def dot(a, b):
    return jnp.dot(a, b, preferred_element_type=f32)


def iota(shape, dim):
    return lax.broadcasted_iota(i32, shape, dim)


def call(kernel, outs, args, flops, scratch=(), aliases={}, limit=20 << 20):
    moved = sum(x.size * x.dtype.itemsize for x in (*args, *outs))
    return pl.pallas_call(
        kernel,
        out_shape=outs,
        in_specs=[pl.BlockSpec(memory_space=pltpu.VMEM)] * len(args),
        out_specs=tuple(pl.BlockSpec(memory_space=pltpu.VMEM) for _ in outs),
        scratch_shapes=scratch,
        input_output_aliases=aliases,
        compiler_params=pltpu.CompilerParams(vmem_limit_bytes=limit),
        cost_estimate=pl.CostEstimate(flops=flops, bytes_accessed=moved, transcendentals=0),
    )(*args)


def shape(dims, dtype):
    return jax.ShapeDtypeStruct(dims, dtype)


def join_kernel(first_ref, second_ref, out_ref, sems):
    copies = [
        pltpu.make_async_copy(ref.at[0], out_ref.at[k], sems.at[k])
        for k, ref in enumerate((first_ref, second_ref))
    ]
    for copy in copies:
        copy.start()
    for copy in copies:
        copy.wait()


def front_kernel(taps, x_ref, low_ref, high_ref, kernel_ref, gain_ref, router_ref, routes_ref,
                 sent_ref, res_ref, high_w_ref, low_w_ref, high_x_ref, low_x_ref, padded, kernels):
    tok, features = x_ref.shape
    tiles = features // LANES
    skip = HALO - (taps - 1) // 2
    for c in range(tiles):
        cols = slice(c * LANES, (c + 1) * LANES)
        padded[c, :HALO] = low_ref[:, cols].astype(f32)
        padded[c, HALO : HALO + tok] = x_ref[:, cols].astype(f32)
        padded[c, HALO + tok :] = high_ref[:, cols].astype(f32)
        kernels[c, :taps] = kernel_ref[:, cols].astype(f32)

    def column(c, squares):
        acc = jnp.zeros((tok, LANES), f32)
        for j in range(taps):
            acc = acc + kernels[c, pl.ds(j, 1), :] * padded[c, pl.ds(j + skip, tok), :]
        res = padded[c, pl.ds(HALO, tok), :] + acc / (1.0 + jnp.exp(-acc))
        res_ref[:, pl.ds(pl.multiple_of(c * LANES, LANES), LANES)] = res
        return squares + res * res

    squares = lax.fori_loop(0, tiles, column, jnp.zeros((tok, LANES), f32))
    mean = jnp.sum(squares, axis=-1, keepdims=True) / features
    scale = lax.rsqrt(mean + 1e-06)
    normed = (res_ref[...] * scale * gain_ref[...].astype(f32)).astype(bf16)

    experts = router_ref.shape[0]
    rows = experts * MAIN
    expert_of = iota((experts, tok), 0)
    hots = [(expert_of == routes_ref[k : k + 1, :]).astype(f32) for k in range(2)]
    before = (iota((tok, tok), 0) < iota((tok, tok), 1)).astype(bf16)
    counts = dot((hots[0] + hots[1]).astype(bf16), before)
    logits = lax.dot_general(router_ref[...], normed, TRANSPOSED, preferred_element_type=f32)
    place = iota((rows, tok), 0)
    main = jnp.zeros((rows, tok), f32)
    extra = jnp.zeros((rows, tok), f32)
    main_w = jnp.zeros((rows, tok), f32)
    extra_w = jnp.zeros((rows, tok), f32)
    for k in range(2):
        slot = jnp.sum(counts * hots[k], axis=0, keepdims=True).astype(i32)
        logit = jnp.sum(logits * hots[k], axis=0, keepdims=True)
        gate = 1.0 / (1.0 + jnp.exp(-logit))
        expert = routes_ref[k : k + 1, :]
        inside = slot < MAIN
        first = jnp.where(inside, expert * MAIN + slot, -1)
        hit = place == first
        main = main + hit.astype(f32)
        main_w = main_w + jnp.where(hit, gate, 0.0)
        last = jnp.where(inside, -1, expert)
        hit = lax.shift_right_arithmetic(place, 3) == last
        extra = extra + hit.astype(f32)
        extra_w = extra_w + jnp.where(hit, gate, 0.0)
    sent_ref[:, :features] = dot(main.astype(bf16), normed).astype(bf16)
    pieces = jnp.zeros((rows, WIDE), f32)
    piece_of = jnp.bitwise_and(place, MAIN - 1)
    for j in range(features // WIDE):
        chosen = jnp.where(piece_of == j, extra, 0.0).astype(bf16)
        pieces = pieces + dot(chosen, normed[:, j * WIDE : (j + 1) * WIDE])
    sent_ref[:, features:] = pieces.astype(bf16)
    for weights, high, low in ((main_w, high_w_ref, low_w_ref), (extra_w, high_x_ref, low_x_ref)):
        turned = weights.T
        coarse = turned.astype(bf16)
        high[...] = coarse
        low[...] = (turned - coarse.astype(f32)).astype(bf16)


def front(x, low, high, kernel, gain, router, routes):
    tok, features = x.shape
    taps = kernel.shape[0]
    rows = router.shape[0] * MAIN
    outs = (
        shape((rows, features + WIDE), bf16),
        shape((tok, features), f32),
        *(shape((tok, rows), bf16) for _ in range(4)),
    )
    tiles = features // LANES
    return call(
        functools.partial(front_kernel, taps),
        outs,
        (x, low, high, kernel, gain, router, routes),
        flops=20_000_000_000,
        scratch=[pltpu.VMEM((tiles, tok + 2 * HALO, LANES), f32), pltpu.VMEM((tiles, 32, LANES), f32)],
    )


def ffn(rows, blocks):
    whole = [b for b in blocks if len(b.shape) == 3]
    split = [b for b in blocks if len(b.shape) == 2]
    first = jnp.concatenate([b[0] for b in whole] + [b[...] for b in split[::2]], axis=0)
    second = jnp.concatenate([b[1] for b in whole] + [b[...] for b in split[1::2]], axis=0)
    preact = lax.dot_general(rows, first, TRANSPOSED, preferred_element_type=f32)
    hidden = (preact / (1.0 + jnp.exp(-preact))).astype(bf16)
    return hidden, second


def unpacked(packed_ref, rows_ref, base, features):
    count = packed_ref.shape[0]
    experts = count // MAIN
    rows_ref[base : base + count] = packed_ref[:, :features]
    pieces = packed_ref[:, features:]
    for j in range(features // WIDE):
        pick = (iota((experts, count), 1) == iota((experts, count), 0) * MAIN + j).astype(bf16)
        rows_ref[base + count : base + count + experts, j * WIDE : (j + 1) * WIDE] = dot(pick, pieces).astype(bf16)


def accumulate(hidden, second, out_ref, old_ref=None):
    for n in range(0, second.shape[1], 512):
        part = dot(hidden, second[:, n : n + 512])
        out_ref[:, n : n + 512] = part if old_ref is None else old_ref[:, n : n + 512] + part


def begin_kernel(mine_ref, other_ref, *refs):
    *blocks, rows_ref, total_ref = refs
    features = rows_ref.shape[1]
    unpacked(mine_ref, rows_ref, 0, features)
    unpacked(other_ref, rows_ref, rows_ref.shape[0] // 2, features)
    hidden, second = ffn(rows_ref[...], blocks)
    accumulate(hidden, second, total_ref)


def more_kernel(rows_ref, old_ref, *refs):
    *blocks, total_ref = refs
    hidden, second = ffn(rows_ref[...], blocks)
    accumulate(hidden, second, total_ref, old_ref)


def end_kernel(own_rows, rows_ref, old_ref, *refs):
    *blocks, out_ref = refs
    half = rows_ref.shape[0] // 2
    here = slice(0, half) if own_rows else slice(half, 2 * half)
    hidden, second = ffn(rows_ref[here], blocks)
    for n in range(0, second.shape[1], 512):
        part = old_ref[here, n : n + 512] + dot(hidden, second[:, n : n + 512])
        out_ref[:, n : n + 512] = part.astype(out_ref.dtype)


def pack_kernel(mine_ref, other_ref, packed_ref):
    count, features = packed_ref.shape[0], mine_ref.shape[1]
    experts = count // MAIN
    summed = (mine_ref[...] + other_ref[...].astype(f32)).astype(bf16)
    packed_ref[:, :features] = summed[:count]
    extra = summed[count:]
    pieces = jnp.zeros((count, WIDE), f32)
    for j in range(features // WIDE):
        place = (iota((count, experts), 0) == iota((count, experts), 1) * MAIN + j).astype(bf16)
        pieces = pieces + dot(place, extra[:, j * WIDE : (j + 1) * WIDE])
    packed_ref[:, features:] = pieces.astype(bf16)


def combine_kernel(back_ref, res_ref, high_w_ref, low_w_ref, high_x_ref, low_x_ref, out_ref):
    tok, features = res_ref.shape
    count = back_ref.shape[0]
    pieces = back_ref[:, features:]
    piece_of = jnp.bitwise_and(iota((tok, count), 1), MAIN - 1)
    for j in range(features // WIDE):
        cols = slice(j * WIDE, (j + 1) * WIDE)
        here = piece_of == j
        back = back_ref[:, cols]
        pulled = dot(high_w_ref[...], back) + dot(low_w_ref[...], back)
        for ref in (high_x_ref, low_x_ref):
            weights = jnp.where(here, ref[...].astype(f32), 0.0).astype(bf16)
            pulled = pulled + dot(weights, pieces)
        out_ref[:, cols] = (res_ref[:, cols] + pulled).astype(bf16)


def shards(frames_in, conv_kernel, norm_gain, router, w_in, w_out, routes):
    tok, features = frames_in.shape[1:]
    experts = router.shape[1]
    dp = lax.axis_size("dp")
    chips = dp // 2
    up = [(i, (i + 2) % dp) for i in range(dp)]
    down = [(i, (i - 2) % dp) for i in range(dp)]
    sibling = [(i, i ^ 1) for i in range(dp)]
    frames = frames_in[0]

    low = lax.ppermute(frames[tok - HALO :], "dp", [(i, i + 1) for i in range(dp - 1)])
    high = lax.ppermute(frames[:HALO], "dp", [(i + 1, i) for i in range(dp - 1)])

    units = w_in.shape[1]
    own = pl.pallas_call(
        join_kernel,
        out_shape=shape((2, *w_in.shape[1:]), bf16),
        in_specs=[pl.BlockSpec(memory_space=pl.ANY)] * 2,
        out_specs=pl.BlockSpec(memory_space=pltpu.VMEM),
        scratch_shapes=[pltpu.SemaphoreType.DMA((2,))],
    )(w_in, w_out)
    a1, b1 = lax.ppermute(own, "dp", up), lax.ppermute(own, "dp", down)

    def step(ups, downs):
        moved = [(lax.ppermute(a, "dp", up), lax.ppermute(b, "dp", down)) for a, b in zip(ups, downs)]
        return [m[0] for m in moved], [m[1] for m in moved]

    a2, b2 = step([a1[0], a1[1]], [b1[0], b1[1]])
    a3, b3 = step(a2, b2)
    sent, residual, *weights = front(
        frames, low, high, conv_kernel, norm_gain[None], router.T, routes[0].T
    )
    assert chips == 8

    def exchange(v):
        parts = v.reshape(experts, MAIN, v.shape[1])
        out = lax.all_to_all(parts, "expert", split_axis=0, concat_axis=0, tiled=True)
        return out.reshape(v.shape)

    mine = exchange(sent)
    other = lax.ppermute(mine, "dp", sibling)
    count = experts * (MAIN + 1)
    flops = lambda units: 2 * 2 * 2 * count * units * features
    rows, total = call(
        begin_kernel,
        (shape((2 * count, features), bf16), shape((2 * count, features), f32)),
        (mine, other, own, a1, b1, *a2, *b2),
        flops(5 * units),
    )
    total, a3[0], b3[0] = lax.optimization_barrier((total, a3[0], b3[0]))
    half = units // 2
    a4, b4 = step([a[:half] for a in a3], [b[half:] for b in b3])
    (total,) = call(
        more_kernel, (shape(total.shape, f32),), (rows, total, *a3, *b3), flops(2 * units), aliases={1: 0}
    )
    (gone,) = call(
        functools.partial(end_kernel, False),
        (shape((count, features), bf16),),
        (rows, total, *a4, *b4),
        flops(units) // 2,
    )
    came = lax.ppermute(gone, "dp", sibling)
    (kept,) = call(
        functools.partial(end_kernel, True),
        (shape((count, features), f32),),
        (rows, total, *a4, *b4),
        flops(units) // 2,
    )
    (packed,) = call(pack_kernel, (shape(sent.shape, bf16),), (kept, came), 10_000_000)
    back = exchange(packed)
    (out,) = call(combine_kernel, (shape((tok, features), bf16),), (back, residual, *weights), 10_000_000)
    return out[None]


def solution(mesh):
    rows = P("expert", "dp", None)
    return jax.shard_map(
        shards,
        mesh=mesh,
        in_specs=(rows, P(), P(), P(), rows, rows, rows),
        out_specs=rows,
        check_vma=False,
    )
```
